512 devices in a mesh: space: 32 (over y, x, core), blk: 16 (over z).
Axes of the slice: x: 4, y: 4, z: 16, core: 2. Of those that a mesh axis runs over, the one named last changes fastest.
Arguments:
- snapshots: bfloat16 [20480, 16384], P('blk', 'space'), may hold values from -6 to 6
- row_scales: float32 [20480], P('blk'), may hold values from 0.3 to 3
- block_offsets: int32 [64], P('blk'), may hold values from 0 to 768, as said below
- freq_index: int32 [16], replicated, may hold values from 1 to 255
Outputs:
- modes: float32 [16, 16384, 128], P('blk', 'space')
- r_factor: float32 [16, 2, 64, 64], P('blk')
The draws below stay inside these ranges and needn't reach their ends.
Inputs may be any that keep to these rules, and one draw needn't show every extreme that they name: `block_offsets`: block offsets index the snapshots held by the block's own index of blk; within every group of 4 blocks they are distinct and increasing, block i of a group lies between i * 256 - 512 / 4 and i * 256 + 512 / 4; in the first group the first is 0 and the last is 768.
All inputs are finite; a program needn't handle non-finite values.
Results may differ from the reference program's by a relative error of at most 0.0064.
Values may be sent and summed in bfloat16 or wider, within the bound.
A program may use at most 64 MiB of HBM per device.

```python
import math
import jax
import jax.numpy as jnp
from jax import lax

NFFT = 512
BLK_DEV = 4
FREQS = 16
BLOCKS = 64
SNAP_DEV = 1280
SNAPS = 20480
POINTS = 16384


def draw_block_offsets(key, part):
    groups = BLOCKS // BLK_DEV
    top = SNAP_DEV - NFFT
    jitter = jax.random.randint(key, (groups, BLK_DEV), 0, NFFT // 4, dtype=jnp.int32)
    base = jnp.arange(BLK_DEV, dtype=jnp.int32) * (NFFT // 2)
    values = base[None, :] + jitter
    values = values.at[:, BLK_DEV - 1].set(top - jitter[:, BLK_DEV - 1])
    values = values.at[0, 0].set(0)
    values = values.at[0, BLK_DEV - 1].set(top)
    return values.reshape(BLOCKS).astype(jnp.int32)


def plant(values, key, least, top_value):
    longest = values.shape.index(max(values.shape))
    spots = []
    for shift in (0, 1):
        where = [jax.random.randint(jax.random.fold_in(key, axis), (), 0, length) for axis, length in enumerate(values.shape)]
        where[longest] = (where[longest] + shift) % values.shape[longest]
        spots.append(tuple(where))
    return values.at[spots[0]].set(least).at[spots[1]].set(top_value)


def levels(own_key, extent, split, low, largest):
    gain = 1.0
    for axis_at, shards_of in split:
        steps = jax.random.uniform(jax.random.fold_in(jax.random.fold_in(own_key, 6), axis_at), (shards_of,), jnp.float32, low / len(split), largest / len(split))
        gain = gain * jnp.repeat(jnp.exp(steps), extent[axis_at] // shards_of).reshape((-1,) + (1,) * (len(extent) - 1 - axis_at))
    return gain


def noise(rng, extent, scale, reach, split=(), kind=jnp.bfloat16):
    factor_of = levels(rng, extent, split, -0.22, 0.18) if split else 1.0
    drawn = jax.random.normal(rng, extent, jnp.float32) * scale * factor_of
    return jnp.minimum(jnp.maximum(drawn, -reach), reach).astype(kind)


def setup_inputs(seed: int = 0) -> dict:
    arg_keys = jax.random.split(jax.random.key(seed), 5)
    snapshots = noise(arg_keys[0], (SNAPS, POINTS), 1.0, 6.0, ((0, 16), (1, 32)))
    row_scales = jnp.clip(jnp.exp(math.log(3.0) - 2.3025851 * jax.random.uniform(arg_keys[1], (SNAPS,), jnp.float32) ** levels(arg_keys[1], (SNAPS,), ((0, 16),), -0.2, 0.2)), 0.3, 3.0)
    block_offsets = draw_block_offsets(jax.random.fold_in(arg_keys[4], 71), 0)
    freq_index = plant(jax.random.randint(arg_keys[3], (FREQS,), 1, NFFT // 2), jax.random.fold_in(arg_keys[3], 1), 1, (NFFT // 2) - 1).astype(jnp.int32)
    return dict(snapshots=snapshots, row_scales=row_scales, block_offsets=block_offsets, freq_index=freq_index)


def trig_table(freq_index):
    times = jnp.arange(NFFT, dtype=jnp.int32)
    phase = freq_index[:, None] * times[None, :] % NFFT
    angle = 2.0 * math.pi / NFFT * phase.astype(jnp.float32)
    inv_root = 1.0 / math.sqrt(NFFT)
    table = jnp.stack([jnp.cos(angle), -jnp.sin(angle)], 1).reshape(2 * freq_index.shape[0], NFFT) * inv_root
    hann = 0.5 - 0.5 * jnp.cos(2.0 * math.pi / NFFT * times.astype(jnp.float32))
    return (table, hann)

def reference(snapshots, row_scales, block_offsets, freq_index):
    table, hann = trig_table(freq_index)
    starts = jnp.arange(BLOCKS, dtype=jnp.int32) // BLK_DEV * SNAP_DEV + block_offsets.astype(jnp.int32)

    def one_block(start):
        window = lax.dynamic_slice_in_dim(snapshots, start, NFFT, 0)
        scaled = lax.dynamic_slice_in_dim(row_scales, start, NFFT, 0)
        coef = (table * (hann * scaled)[None, :]).astype(jnp.bfloat16)
        return jnp.dot(coef.astype(jnp.float32), window.astype(jnp.float32), preferred_element_type=jnp.float32).astype(jnp.bfloat16)
    spectra = lax.map(one_block, starts)
    spectra = spectra.reshape(BLOCKS, FREQS, 2, POINTS).transpose(1, 3, 0, 2).reshape(FREQS, POINTS, 2 * BLOCKS)

    def per_freq(single):
        pairs = single.reshape(POINTS, BLOCKS, 2)
        rotated = jnp.stack([-pairs[:, :, 1], pairs[:, :, 0]], -1).reshape(POINTS, 2 * BLOCKS)
        stacked = jnp.concatenate([single, rotated], 0)
        gram = jnp.dot(stacked.T.astype(jnp.float32), stacked.astype(jnp.float32), preferred_element_type=jnp.float32) / POINTS
        lower_factor = jnp.linalg.cholesky(gram)
        upper = lower_factor.T
        solved = jax.scipy.linalg.solve_triangular(lower_factor, single.astype(jnp.float32).T, lower=True)
        r_pair = jnp.stack([upper[0::2, 0::2], upper[0::2, 1::2]], 0)
        return (solved.T, r_pair)
    modes, r_factor = lax.map(per_freq, spectra)
    return (modes, r_factor)
```

```python
import math

import jax
import jax.numpy as jnp
from jax import lax
from jax.sharding import PartitionSpec as P

NFFT = 512


def padded_coeffs(row_scales, block_offsets, freq_index):
    rows = row_scales.shape[0]
    times = jnp.arange(rows, dtype=jnp.int32)[None, :] - block_offsets[:, None]
    inside = (times >= 0) & (times < NFFT)
    hann = 0.5 - 0.5 * jnp.cos(2.0 * math.pi / NFFT * times.astype(jnp.float32))
    weight = jnp.where(inside, hann * row_scales[None, :], 0.0) / math.sqrt(NFFT)
    quarter = jnp.arange(2, dtype=jnp.int32) * (NFFT // 4)
    phase = freq_index[:, None, None, None] * times[None, :, None, :]
    phase = (phase + quarter[None, None, :, None]) & (NFFT - 1)
    table = jnp.cos(2.0 * math.pi / NFFT * phase.astype(jnp.float32))
    return (table * weight[None, :, None, :]).astype(jnp.bfloat16)


def local(snapshots, row_scales, block_offsets, freq_index):
    points_here = snapshots.shape[1]
    freq_count = freq_index.shape[0]
    blocks_here = block_offsets.shape[0]
    coeffs = padded_coeffs(row_scales, block_offsets, freq_index)
    coeffs = coeffs.reshape(freq_count * blocks_here * 2, -1)
    spectra = jnp.dot(coeffs, snapshots, preferred_element_type=jnp.float32)
    spectra = spectra.astype(jnp.bfloat16).reshape(freq_count, 2 * blocks_here, points_here)
    regrouped = lax.all_to_all(spectra, "blk", split_axis=0, concat_axis=1, tiled=True)
    rows = regrouped[0]
    total_points = points_here * lax.axis_size("space")
    product = jnp.dot(rows, rows.T, preferred_element_type=jnp.float32) / total_points
    product = lax.optimization_barrier(lax.psum(product, "space"))
    width = product.shape[0]
    quads = product.reshape(width // 2, 2, width // 2, 2)
    real = quads[:, 0, :, 0] + quads[:, 1, :, 1]
    imag = quads[:, 0, :, 1] - quads[:, 1, :, 0]
    gram = jnp.stack(
        [jnp.stack([real, imag], -1), jnp.stack([-imag, real], -1)], 1
    ).reshape(width, width)
    lower = jnp.linalg.cholesky(gram)
    identity = jnp.eye(width, dtype=jnp.float32)
    inverse_lower = jax.scipy.linalg.solve_triangular(lower, identity, lower=True)
    modes = lax.dot_general(
        rows.astype(jnp.float32),
        inverse_lower,
        (((0,), (1,)), ((), ())),
        precision=lax.Precision.HIGHEST,
    )
    upper = lower.T
    r_factor = jnp.stack([upper[0::2, 0::2], upper[0::2, 1::2]], 0)
    return (modes[None], r_factor[None])


def solution(mesh):
    return jax.shard_map(
        local,
        mesh=mesh,
        in_specs=(P("blk", "space"), P("blk"), P("blk"), P()),
        out_specs=(P("blk", "space", None), P("blk", None, None, None)),
        check_vma=False,
    )
```

```python
import functools
import math

import jax
import jax.numpy as jnp
from jax import lax
from jax.experimental import pallas as pl
from jax.experimental.pallas import tpu as pltpu
from jax.sharding import PartitionSpec as P

NFFT = 512
TILE = 8
LANES = 128
MESH = pl.DeviceIdType.MESH


def cos_turns(turns):
    frac = turns - jnp.floor(turns + 0.5)
    half = frac * math.pi
    sq = half * half
    poly = 1.0 + sq * (
        -1.0 / 6
        + sq
        * (
            1.0 / 120
            + sq * (-1.0 / 5040 + sq * (1.0 / 362880 + sq * (-1.0 / 39916800 + sq * (1.0 / 6227020800))))
        )
    )
    sine = half * poly
    return 1.0 - 2.0 * (sine * sine)


def grid_of(space):
    side = {32: 4, 8: 2}[space]
    return side, side


def gather_kernel(
    sides, zs, total_points,
    snaps_hbm, scales_ref, offs_ref, freq_ref,
    xy_ref, gram_ref,
    snaps, coef, send, recv, rows32, pair_buf, x_buf, y_buf,
    load_sem, send_sems, recv_sems, gsend_sems, grecv_sems,
):
    ys, xs = sides
    z = lax.axis_index("blk")
    s = lax.axis_index("space")
    core = lax.rem(s, 2)
    x = lax.rem(s // 2, xs)
    y = s // (2 * xs)

    load = pltpu.make_async_copy(snaps_hbm, snaps, load_sem)
    load.start()

    def space_of(yy, xx, cc):
        return (yy * xs + xx) * 2 + cc

    z_peers = [lax.rem(z + d, zs) for d in range(1, zs)]
    x_peers = [space_of(y, lax.rem(x + d, xs), core) for d in range(1, xs)]
    y_peers = [space_of(lax.rem(y + d, ys), x, core) for d in range(1, ys)]
    pair = space_of(y, x, 1 - core)

    barrier = pltpu.get_barrier_semaphore()
    for peer in z_peers:
        pl.semaphore_signal(barrier, inc=1, device_id={"blk": peer}, device_id_type=MESH)
    for peer in [pair] + x_peers + y_peers:
        pl.semaphore_signal(barrier, inc=1, device_id={"space": peer}, device_id_type=MESH)

    rows = snaps.shape[0]
    freqs = freq_ref.shape[0]
    sub = lax.broadcasted_iota(jnp.int32, (TILE, rows), 0)
    times = lax.broadcasted_iota(jnp.int32, (TILE, rows), 1)
    start = jnp.full((TILE, rows), offs_ref[0], jnp.int32)
    for b in range(1, TILE // 2):
        start = jnp.where(sub >= 2 * b, offs_ref[b], start)
    times = times - start
    ftimes = times.astype(jnp.float32)
    hann = 0.5 - 0.5 * cos_turns(ftimes * (1.0 / NFFT))
    inside = (times >= 0) & (times < NFFT)
    weight = jnp.where(inside, hann * scales_ref[...], 0.0) * (1.0 / math.sqrt(NFFT))
    quarter = (sub & 1).astype(jnp.float32) * 0.25

    def rows_of(j):
        turns = ftimes * (freq_ref[j].astype(jnp.float32) * (1.0 / NFFT)) + quarter
        return cos_turns(turns) * weight

    @pl.loop(0, freqs // 2)
    def _(jj):
        both = jnp.concatenate([rows_of(2 * jj), rows_of(2 * jj + 1)], 0)
        coef[pl.ds(pl.multiple_of(jj * 16, 16), 16), :] = both.astype(jnp.bfloat16)

    load.wait()
    spectra = jnp.dot(coef[...], snaps[...], preferred_element_type=jnp.float32)
    send[...] = spectra.reshape(send.shape).astype(jnp.bfloat16)
    recv[z] = send[z]

    pl.semaphore_wait(barrier, len(z_peers) + 1 + len(x_peers) + len(y_peers))
    order = sorted(range(1, zs), key=lambda d: -min(d, zs - d))
    copies = []
    for d in order:
        peer = z_peers[d - 1]
        copy = pltpu.make_async_remote_copy(
            src_ref=send.at[peer],
            dst_ref=recv.at[z],
            send_sem=send_sems.at[d],
            recv_sem=recv_sems.at[d],
            device_id={"blk": peer},
            device_id_type=MESH,
        )
        copy.start()
        copies.append(copy)
    for copy in copies:
        copy.wait_recv()
    points = recv.shape[2]
    half = zs * TILE // 2
    chunks = range(points // LANES)
    for q in chunks:
        part = recv[:, :, LANES * q : LANES * (q + 1)].astype(jnp.float32)
        rows32[q] = part.reshape(2 * half, LANES)

    def every_other(first):
        parts = [rows32[q, pl.ds(first, half, stride=2), :] for q in chunks]
        return jnp.concatenate(parts, 1).astype(jnp.bfloat16)

    re, im = every_other(0), every_other(1)
    xy_ref[pl.ds(0, half), :] = re
    xy_ref[pl.ds(half, half), :] = im
    left = jnp.concatenate([re, im], 1)
    right = jnp.concatenate([left, jnp.concatenate([im, -re], 1)], 0)
    gram = lax.dot_general(
        left, right, (((1,), (1,)), ((), ())), preferred_element_type=jnp.float32
    )
    pair_buf[core] = gram
    for copy in copies:
        copy.wait_send()

    def exchange(buf, here, peers, base):
        moves = []
        for i, peer in enumerate(peers):
            move = pltpu.make_async_remote_copy(
                src_ref=buf.at[here],
                dst_ref=buf.at[here],
                send_sem=gsend_sems.at[base + i],
                recv_sem=grecv_sems.at[base + i],
                device_id={"space": peer},
                device_id_type=MESH,
            )
            move.start()
            moves.append(move)
        for move in moves:
            move.wait()
        total = buf[0]
        for i in range(1, buf.shape[0]):
            total = total + buf[i]
        return total

    x_buf[x] = exchange(pair_buf, core, [pair], 0)
    y_buf[y] = exchange(x_buf, x, x_peers, 1)
    gram_ref[...] = exchange(y_buf, y, y_peers, xs) * (1.0 / total_points)


def gather_call(snapshots, scales, offsets, freqs, *, space, zs):
    sides = grid_of(space)
    points = snapshots.shape[1]
    cols = zs * TILE
    kernel = functools.partial(gather_kernel, sides, zs, points * space)
    gram_shape = (cols // 2, cols)
    vmem = pl.BlockSpec(memory_space=pltpu.VMEM)
    smem = pl.BlockSpec(memory_space=pltpu.SMEM)
    return pl.pallas_call(
        kernel,
        out_shape=(
            jax.ShapeDtypeStruct((cols, points), jnp.bfloat16),
            jax.ShapeDtypeStruct(gram_shape, jnp.float32),
        ),
        in_specs=[pl.BlockSpec(memory_space=pl.ANY), vmem, smem, smem],
        out_specs=(vmem, vmem),
        scratch_shapes=[
            pltpu.VMEM(snapshots.shape, jnp.bfloat16),
            pltpu.VMEM((zs * TILE, snapshots.shape[0]), jnp.bfloat16),
            pltpu.VMEM((zs, TILE, points), jnp.bfloat16),
            pltpu.VMEM((zs, TILE, points), jnp.bfloat16),
            pltpu.VMEM((points // LANES, cols, LANES), jnp.float32),
            pltpu.VMEM((2,) + gram_shape, jnp.float32),
            pltpu.VMEM((sides[1],) + gram_shape, jnp.float32),
            pltpu.VMEM((sides[0],) + gram_shape, jnp.float32),
            pltpu.SemaphoreType.DMA(()),
            pltpu.SemaphoreType.DMA((zs,)),
            pltpu.SemaphoreType.DMA((zs,)),
            pltpu.SemaphoreType.DMA((sum(sides),)),
            pltpu.SemaphoreType.DMA((sum(sides),)),
        ],
        compiler_params=pltpu.CompilerParams(collective_id=0, has_side_effects=True),
        name="spectra_and_gram",
    )(snapshots, scales, offsets, freqs)


def factor_kernel(xy_ref, gram_ref, modes_ref, r_ref, w_ref):
    n = gram_ref.shape[0]
    width = 2 * n
    tiles = n // TILE
    lane = lax.broadcasted_iota(jnp.int32, (TILE, width), 1)
    sub = lax.broadcasted_iota(jnp.int32, (TILE, width), 0)
    sign = jnp.where(lane < n, -1.0, 1.0)

    def turn(value):
        return pltpu.roll(value, n, 1) * sign

    def spread(value, row):
        return jnp.broadcast_to(value[row : row + 1, :], (TILE, width))

    def across(value, column):
        return jnp.broadcast_to(value[:, column : column + 1], (TILE, width))

    cs = [gram_ref[pl.ds(TILE * i, TILE), :] for i in range(tiles)]
    ls = [jnp.where(lane == sub + TILE * i, 1.0, 0.0) for i in range(tiles)]

    for panel in range(tiles):
        group = [panel] + ([panel + 1] if panel + 1 < tiles else [])
        res = {i: [across(cs[i], TILE * panel + j) for j in range(TILE)] for i in group}
        ims = {i: [across(cs[i], n + TILE * panel + j) for j in range(TILE)] for i in group}
        scale = jnp.zeros((TILE, width), jnp.float32)
        for k in range(TILE):
            pivot = spread(res[panel][k], k)
            inverse = 1.0 / pivot
            scale = jnp.where(sub == k, lax.rsqrt(pivot), scale)
            mults = {}
            for i in group:
                mr, mi = res[i][k] * inverse, ims[i][k] * inverse
                if i == panel:
                    mr = jnp.where(sub > k, mr, 0.0)
                    mi = jnp.where(sub > k, mi, 0.0)
                mults[i] = (mr, mi)
            for j in range(k + 1, TILE):
                pr, pi = spread(res[panel][j], k), spread(ims[panel][j], k)
                for i in group:
                    mr, mi = mults[i]
                    res[i][j] = res[i][j] - (mr * pr - mi * pi)
                    ims[i][j] = ims[i][j] - (mr * pi + mi * pr)
            c_row, l_row = spread(cs[panel], k), spread(ls[panel], k)
            c_turn, l_turn = turn(c_row), turn(l_row)
            for i in group:
                mr, mi = mults[i]
                cs[i] = cs[i] - (mr * c_row + mi * c_turn)
                ls[i] = ls[i] - (mr * l_row + mi * l_turn)
        r_rows = cs[panel] * scale
        l_rows = ls[panel] * scale
        if panel + 2 < tiles:
            first = TILE * (panel + 2)
            lhs = jnp.concatenate([r_rows, pltpu.roll(r_rows, n, 1)], 0)
            rhs = jnp.concatenate(
                [
                    jnp.concatenate([r_rows, l_rows], 1),
                    jnp.concatenate([-turn(r_rows), -turn(l_rows)], 1),
                ],
                0,
            )
            update = lax.dot_general(
                lhs[:, :n],
                rhs,
                (((0,), (0,)), ((), ())),
                precision=lax.Precision.HIGHEST,
                preferred_element_type=jnp.float32,
            )
            for i in range(panel + 2, tiles):
                part = update[TILE * i : TILE * (i + 1), :]
                cs[i] = cs[i] - part[:, :width]
                ls[i] = ls[i] - part[:, width:]
        row = sub + TILE * panel
        keep = (lane >= row) & ((lane < n) | (lane - n > row))
        r_rows = jnp.where(keep, r_rows, 0.0)
        r_ref[0, pl.ds(TILE * panel, TILE), :] = r_rows[:, :n]
        r_ref[1, pl.ds(TILE * panel, TILE), :] = pltpu.roll(r_rows, n, 1)[:, :n]
        w_ref[pl.ds(2 * TILE * panel, TILE, stride=2), :] = l_rows
        w_ref[pl.ds(2 * TILE * panel + 1, TILE, stride=2), :] = turn(l_rows)

    w = w_ref[...]
    high = w.astype(jnp.bfloat16)
    low = (w - high.astype(jnp.float32)).astype(jnp.bfloat16)
    xy = xy_ref[...]
    dims = (((0,), (1,)), ((), ()))
    modes = lax.dot_general(xy, high, dims, preferred_element_type=jnp.float32)
    modes += lax.dot_general(xy, low, dims, preferred_element_type=jnp.float32)
    modes_ref[...] = modes


def factor_call(xy, gram):
    n = gram.shape[0]
    return pl.pallas_call(
        factor_kernel,
        out_shape=(
            jax.ShapeDtypeStruct((xy.shape[1], 2 * n), jnp.float32),
            jax.ShapeDtypeStruct((2, n, n), jnp.float32),
        ),
        scratch_shapes=[pltpu.VMEM((2 * n, 2 * n), jnp.float32)],
        name="factor_and_modes",
    )(xy, gram)


def local(space, zs, snapshots, row_scales, block_offsets, freq_index):
    xy, gram = gather_call(
        snapshots, row_scales[None, :], block_offsets, freq_index, space=space, zs=zs
    )
    modes, r_factor = factor_call(xy, gram)
    return (modes[None], r_factor[None])


def solution(mesh):
    return jax.shard_map(
        functools.partial(local, mesh.shape["space"], mesh.shape["blk"]),
        mesh=mesh,
        in_specs=(P("blk", "space"), P("blk"), P("blk"), P()),
        out_specs=(P("blk", "space", None), P("blk", None, None, None)),
        check_vma=False,
    )
```

```python
import functools
import math

import jax
import jax.numpy as jnp
from jax import lax
from jax.experimental import pallas as pl
from jax.experimental.pallas import tpu as pltpu
from jax.sharding import PartitionSpec as P

NFFT = 512
TILE = 8
LANES = 128
PARTS = 1
MESH = pl.DeviceIdType.MESH


def cos_turns(turns):
    frac = turns - jnp.floor(turns + 0.5)
    half = frac * math.pi
    sq = half * half
    poly = 1.0 + sq * (
        -1.0 / 6
        + sq
        * (
            1.0 / 120
            + sq * (-1.0 / 5040 + sq * (1.0 / 362880 + sq * (-1.0 / 39916800 + sq * (1.0 / 6227020800))))
        )
    )
    sine = half * poly
    return 1.0 - 2.0 * (sine * sine)


def sides_of(space):
    side = {32: 4, 8: 2}[space]
    return side, side


def iota(shape, axis):
    return lax.broadcasted_iota(jnp.int32, shape, axis)


def write_coeffs(scales_ref, offs_ref, freq_ref, coef, table, phase):
    rows = scales_ref.shape[0]
    freqs = freq_ref.shape[0]
    tile = (TILE, LANES)
    sub, lane = iota(tile, 0), iota(tile, 1)
    start = jnp.full(tile, offs_ref[0], jnp.int32)
    for b in range(1, TILE // 2):
        start = jnp.where(sub >= 2 * b, offs_ref[b], start)

    high = (freqs + TILE - 1) // TILE * TILE
    down = jnp.zeros((high, LANES), jnp.float32)
    along = jnp.zeros(tile, jnp.float32)
    for j in range(freqs):
        freq = freq_ref[j].astype(jnp.float32) * (1.0 / NFFT)
        down = jnp.where(iota((high, LANES), 0) == j, freq, down)
        along = jnp.where(lane == j, freq, along)
    for q in range(NFFT // LANES):
        turns = down * (iota((high, LANES), 1) + LANES * q).astype(jnp.float32)
        table[0, q] = cos_turns(turns)
        table[1, q] = cos_turns(turns + 0.25)
    turns = (sub & 1).astype(jnp.float32) * 0.25 - along * start.astype(jnp.float32)
    cos_part, sin_part = cos_turns(turns), cos_turns(turns + 0.25)
    for j in range(freqs):
        phase[0, j] = jnp.broadcast_to(cos_part[:, j : j + 1], tile)
        phase[1, j] = jnp.broadcast_to(sin_part[:, j : j + 1], tile)

    weights = []
    for q in range(rows // LANES):
        times = lane + LANES * q - start
        hann = 0.5 - 0.5 * cos_turns(times.astype(jnp.float32) * (1.0 / NFFT))
        scale = scales_ref[pl.ds(LANES * q, LANES)]
        inside = (times >= 0) & (times < NFFT)
        weight = jnp.where(inside, hann * scale[None, :], 0.0)
        weights.append(weight * (1.0 / math.sqrt(NFFT)))

    @pl.loop(0, freqs // 2)
    def _(pair):
        for q in range(rows // LANES):
            turn = q % (NFFT // LANES)
            parts = []
            for j in (2 * pair, 2 * pair + 1):
                cosine = table[0, turn, pl.ds(j, 1), :]
                sine = table[1, turn, pl.ds(j, 1), :]
                value = cosine * phase[0, j] - sine * phase[1, j]
                parts.append(value * weights[q])
            both = jnp.concatenate(parts, 0).astype(jnp.bfloat16)
            coef[pl.ds(pl.multiple_of(pair * 16, 16), 16), pl.ds(LANES * q, LANES)] = both


def gather_kernel(
    sides, zs, total_points,
    snaps_hbm, scales_hbm, offs_hbm, freq_hbm,
    xy, gram_ref,
    snaps, scales_ref, offs_ref, freq_ref, coef, table, phase, send, recv, rows32,
    pair_buf, x_buf, y_buf,
    load_sems, send_sems, recv_sems, gsend_sems, grecv_sems,
):
    ys, xs = sides
    z = lax.axis_index("blk")
    s = lax.axis_index("space")
    core = lax.rem(s, 2)
    x = lax.rem(s // 2, xs)
    y = s // (2 * xs)

    loads = [
        pltpu.make_async_copy(source, target, load_sems.at[i])
        for i, (source, target) in enumerate(
            [
                (scales_hbm, scales_ref),
                (offs_hbm, offs_ref),
                (freq_hbm, freq_ref),
                (snaps_hbm, snaps),
            ]
        )
    ]
    for load in loads:
        load.start()

    def space_of(yy, xx, cc):
        return (yy * xs + xx) * 2 + cc

    z_peers = [lax.rem(z + d, zs) for d in range(1, zs)]
    x_peers = [space_of(y, lax.rem(x + d, xs), core) for d in range(1, xs)]
    y_peers = [space_of(lax.rem(y + d, ys), x, core) for d in range(1, ys)]
    pair = space_of(y, x, 1 - core)

    barrier = pltpu.get_barrier_semaphore()
    order = sorted(range(1, zs), key=lambda d: -min(d, zs - d))
    for d in order:
        peer = z_peers[d - 1]
        pl.semaphore_signal(barrier, inc=1, device_id={"blk": peer}, device_id_type=MESH)
    for peer in [pair] + x_peers + y_peers:
        pl.semaphore_signal(barrier, inc=1, device_id={"space": peer}, device_id_type=MESH)

    for load in loads[:3]:
        load.wait()
    write_coeffs(scales_ref, offs_ref, freq_ref, coef, table, phase)
    loads[3].wait()
    width = recv.shape[3]
    copies = []
    for h in range(PARTS):
        spectra = jnp.dot(
            coef[...], snaps[:, width * h : width * (h + 1)], preferred_element_type=jnp.float32
        )
        send[h] = spectra.reshape(send.shape[1:]).astype(jnp.bfloat16)
        recv[h, z] = send[h, z]
        if h == 0:
            pl.semaphore_wait(barrier, len(z_peers) + 1 + len(x_peers) + len(y_peers))
        for d in order:
            peer = z_peers[d - 1]
            copy = pltpu.make_async_remote_copy(
                src_ref=send.at[h, peer],
                dst_ref=recv.at[h, z],
                send_sem=send_sems.at[h, d],
                recv_sem=recv_sems.at[h, d],
                device_id={"blk": peer},
                device_id_type=MESH,
            )
            copy.start()
            copies.append(copy)

    half = zs * TILE // 2
    gram = jnp.zeros((half, 2 * half), jnp.float32)
    for h in range(PARTS):
        for copy in copies[(zs - 1) * h : (zs - 1) * (h + 1)]:
            copy.wait_recv()
        chunks = range(width // LANES)
        for q in chunks:
            part = recv[h, :, :, LANES * q : LANES * (q + 1)].astype(jnp.float32)
            rows32[h, q] = part.reshape(2 * half, LANES)

        def every_other(first):
            parts = [rows32[h, q, pl.ds(first, half, stride=2), :] for q in chunks]
            return jnp.concatenate(parts, 1).astype(jnp.bfloat16)

        re, im = every_other(0), every_other(1)
        left = jnp.concatenate([re, im], 1)
        right = jnp.concatenate([left, jnp.concatenate([im, -re], 1)], 0)
        gram += lax.dot_general(
            left, right, (((1,), (1,)), ((), ())), preferred_element_type=jnp.float32
        )
        xy[pl.ds(0, half), pl.ds(width * h, width)] = re
        xy[pl.ds(half, half), pl.ds(width * h, width)] = im

    row, lane = iota(gram.shape, 0), iota(gram.shape, 1)
    packed = jnp.where(lane >= row, gram, pltpu.roll(gram, half, 1))
    upper, lower = packed[: half // 2], pltpu.roll(packed[half // 2 :], half, 1)
    pair_buf[core] = jnp.where(iota(upper.shape, 1) < half, upper, lower)

    def exchange(buf, here, peers, base):
        moves = []
        for i, peer in enumerate(peers):
            move = pltpu.make_async_remote_copy(
                src_ref=buf.at[here],
                dst_ref=buf.at[here],
                send_sem=gsend_sems.at[base + i],
                recv_sem=grecv_sems.at[base + i],
                device_id={"space": peer},
                device_id_type=MESH,
            )
            move.start()
            moves.append(move)
        return moves

    def summed(buf, moves):
        for move in moves:
            move.wait_recv()
        total = buf[0]
        for i in range(1, buf.shape[0]):
            total = total + buf[i]
        return total

    moves_p = exchange(pair_buf, core, [pair], 0)
    x_buf[x] = summed(pair_buf, moves_p)
    moves_x = exchange(x_buf, x, x_peers, 1)
    y_buf[y] = summed(x_buf, moves_x)
    moves_y = exchange(y_buf, y, y_peers, xs)
    for copy in copies + moves_p + moves_x:
        copy.wait_send()
    gram_ref[...] = summed(y_buf, moves_y) * (1.0 / total_points)
    for move in moves_y:
        move.wait_send()


def gather_call(snapshots, scales, offsets, freqs, *, space, zs):
    sides = sides_of(space)
    rows, points = snapshots.shape
    cols = zs * TILE
    width = points // PARTS
    kernel = functools.partial(gather_kernel, sides, zs, points * space)
    gram_shape = (cols // 4, cols)
    vmem = pl.BlockSpec(memory_space=pltpu.VMEM)
    anywhere = pl.BlockSpec(memory_space=pl.ANY)
    high = (zs + TILE - 1) // TILE * TILE
    return pl.pallas_call(
        kernel,
        out_shape=(
            pltpu.VMEM((cols, points), jnp.bfloat16),
            pltpu.VMEM(gram_shape, jnp.float32),
        ),
        in_specs=[anywhere] * 4,
        out_specs=(vmem, vmem),
        scratch_shapes=[
            pltpu.VMEM(snapshots.shape, jnp.bfloat16),
            pltpu.VMEM(scales.shape, jnp.float32),
            pltpu.SMEM(offsets.shape, jnp.int32),
            pltpu.SMEM(freqs.shape, jnp.int32),
            pltpu.VMEM((zs * TILE, rows), jnp.bfloat16),
            pltpu.VMEM((2, NFFT // LANES, high, LANES), jnp.float32),
            pltpu.VMEM((2, zs, TILE, LANES), jnp.float32),
            pltpu.VMEM((PARTS, zs, TILE, width), jnp.bfloat16),
            pltpu.VMEM((PARTS, zs, TILE, width), jnp.bfloat16),
            pltpu.VMEM((PARTS, width // LANES, cols, LANES), jnp.float32),
            pltpu.VMEM((2,) + gram_shape, jnp.float32),
            pltpu.VMEM((sides[1],) + gram_shape, jnp.float32),
            pltpu.VMEM((sides[0],) + gram_shape, jnp.float32),
            pltpu.SemaphoreType.DMA((4,)),
            pltpu.SemaphoreType.DMA((PARTS, zs)),
            pltpu.SemaphoreType.DMA((PARTS, zs)),
            pltpu.SemaphoreType.DMA((sum(sides),)),
            pltpu.SemaphoreType.DMA((sum(sides),)),
        ],
        compiler_params=pltpu.CompilerParams(collective_id=0, has_side_effects=True),
        name="spectra_and_gram",
    )(snapshots, scales, offsets, freqs)


def unpacked(packed, n):
    both = jnp.concatenate([packed, pltpu.roll(packed, n, 1)], 0)
    flipped = both.T
    flipped = flipped[:n, :]
    row, lane = iota((n, n), 0), iota((n, n), 1)
    both = both[:, :n]
    real = jnp.where(lane >= row, both, flipped)
    imag = jnp.where(lane < row, both, jnp.where(lane > row, -flipped, 0.0))
    return jnp.concatenate([real, imag], 1)


def factor_kernel(xy, packed_ref, modes_ref, r_ref, w_ref):
    width = packed_ref.shape[1]
    n = width // 2
    tiles = n // TILE
    gram = unpacked(packed_ref[...], n)
    lane, sub = iota((TILE, width), 1), iota((TILE, width), 0)
    sign = jnp.where(lane < n, -1.0, 1.0)

    def turn(value):
        return pltpu.roll(value, n, 1) * sign

    def spread(value, row):
        return jnp.broadcast_to(value[row : row + 1, :], (TILE, width))

    def across(value, column):
        return jnp.broadcast_to(value[:, column : column + 1], (TILE, width))

    cs = [gram[TILE * i : TILE * (i + 1), :] for i in range(tiles)]
    ls = [jnp.where(lane == sub + TILE * i, 1.0, 0.0) for i in range(tiles)]

    for panel in range(tiles):
        group = [panel] + ([panel + 1] if panel + 1 < tiles else [])
        res = {i: [across(cs[i], TILE * panel + j) for j in range(TILE)] for i in group}
        ims = {i: [across(cs[i], n + TILE * panel + j) for j in range(TILE)] for i in group}
        scale = jnp.zeros((TILE, width), jnp.float32)
        for k in range(TILE):
            pivot = spread(res[panel][k], k)
            inverse = 1.0 / pivot
            scale = jnp.where(sub == k, lax.rsqrt(pivot), scale)
            mults = {i: (res[i][k] * inverse, ims[i][k] * inverse) for i in group}
            for j in range(k + 1, TILE):
                pr, pi = spread(res[panel][j], k), spread(ims[panel][j], k)
                for i in group:
                    mr, mi = mults[i]
                    res[i][j] = res[i][j] - (mr * pr - mi * pi)
                    ims[i][j] = ims[i][j] - (mr * pi + mi * pr)
            c_row, l_row = spread(cs[panel], k), spread(ls[panel], k)
            c_turn, l_turn = turn(c_row), turn(l_row)
            for i in group:
                mr, mi = mults[i]
                if i == panel:
                    mr, mi = jnp.where(sub > k, mr, 0.0), jnp.where(sub > k, mi, 0.0)
                cs[i] = cs[i] - (mr * c_row + mi * c_turn)
                ls[i] = ls[i] - (mr * l_row + mi * l_turn)
        r_rows = cs[panel] * scale
        l_rows = ls[panel] * scale
        if panel + 2 < tiles:
            first = TILE * (panel + 2)
            lhs = jnp.concatenate([r_rows, pltpu.roll(r_rows, n, 1)], 0)
            rhs = jnp.concatenate(
                [
                    jnp.concatenate([r_rows, l_rows], 1),
                    jnp.concatenate([-turn(r_rows), -turn(l_rows)], 1),
                ],
                0,
            )
            update = lax.dot_general(
                lhs[:, :n],
                rhs,
                (((0,), (0,)), ((), ())),
                precision=lax.Precision.HIGHEST,
                preferred_element_type=jnp.float32,
            )
            for i in range(panel + 2, tiles):
                part = update[TILE * i : TILE * (i + 1), :]
                cs[i] = cs[i] - part[:, :width]
                ls[i] = ls[i] - part[:, width:]
        row = sub + TILE * panel
        keep = (lane >= row) & ((lane < n) | (lane - n > row))
        r_rows = jnp.where(keep, r_rows, 0.0)
        r_ref[0, pl.ds(TILE * panel, TILE), :] = r_rows[:, :n]
        r_ref[1, pl.ds(TILE * panel, TILE), :] = pltpu.roll(r_rows, n, 1)[:, :n]
        w_ref[pl.ds(2 * TILE * panel, TILE, stride=2), :] = l_rows
        w_ref[pl.ds(2 * TILE * panel + 1, TILE, stride=2), :] = turn(l_rows)

    w = w_ref[...]
    high = w.astype(jnp.bfloat16)
    low = (w - high.astype(jnp.float32)).astype(jnp.bfloat16)
    points = xy[...]
    dims = (((0,), (1,)), ((), ()))
    modes = lax.dot_general(points, high, dims, preferred_element_type=jnp.float32)
    modes += lax.dot_general(points, low, dims, preferred_element_type=jnp.float32)
    modes_ref[...] = modes


def factor_call(xy, packed):
    width = packed.shape[1]
    n = width // 2
    vmem = pl.BlockSpec(memory_space=pltpu.VMEM)
    return pl.pallas_call(
        factor_kernel,
        out_shape=(
            jax.ShapeDtypeStruct((xy.shape[1], width), jnp.float32),
            jax.ShapeDtypeStruct((2, n, n), jnp.float32),
        ),
        in_specs=[vmem, vmem],
        out_specs=(vmem, vmem),
        scratch_shapes=[
            pltpu.VMEM((width, width), jnp.float32),
        ],
        name="factor_and_modes",
    )(xy, packed)


def local(space, zs, snapshots, row_scales, block_offsets, freq_index):
    xy, packed = gather_call(
        snapshots, row_scales, block_offsets, freq_index, space=space, zs=zs
    )
    xy = pltpu.with_memory_space_constraint(xy, pltpu.VMEM)
    packed = pltpu.with_memory_space_constraint(packed, pltpu.VMEM)
    modes, r_factor = factor_call(xy, packed)
    return (modes[None], r_factor[None])


def solution(mesh):
    return jax.shard_map(
        functools.partial(local, mesh.shape["space"], mesh.shape["blk"]),
        mesh=mesh,
        in_specs=(P("blk", "space"), P("blk"), P("blk"), P()),
        out_specs=(P("blk", "space", None), P("blk", None, None, None)),
        check_vma=False,
    )
```

```python
import functools
import math

import jax
import jax.numpy as jnp
from jax import lax
from jax.experimental import pallas as pl
from jax.experimental.pallas import tpu as pltpu
from jax.sharding import PartitionSpec as P

NFFT = 512
TILE = 8
LANES = 128
PARTS = 1
MESH = pl.DeviceIdType.MESH


def cos_turns(turns):
    frac = turns - jnp.floor(turns + 0.5)
    half = frac * math.pi
    sq = half * half
    poly = 1.0 + sq * (
        -1.0 / 6
        + sq
        * (
            1.0 / 120
            + sq * (-1.0 / 5040 + sq * (1.0 / 362880 + sq * (-1.0 / 39916800 + sq * (1.0 / 6227020800))))
        )
    )
    sine = half * poly
    return 1.0 - 2.0 * (sine * sine)


def sides_of(space):
    side = {32: 4, 8: 2, 2: 1}[space]
    return side, side


def iota(shape, axis):
    return lax.broadcasted_iota(jnp.int32, shape, axis)


def write_coeffs(scales_ref, offs_ref, freq_ref, coef, table, phase):
    rows = scales_ref.shape[0]
    freqs = freq_ref.shape[0]
    tile = (TILE, LANES)
    sub, lane = iota(tile, 0), iota(tile, 1)
    start = jnp.full(tile, offs_ref[0], jnp.int32)
    for b in range(1, TILE // 2):
        start = jnp.where(sub >= 2 * b, offs_ref[b], start)

    high = (freqs + TILE - 1) // TILE * TILE
    down = jnp.zeros((high, LANES), jnp.float32)
    along = jnp.zeros(tile, jnp.float32)
    for j in range(freqs):
        freq = freq_ref[j].astype(jnp.float32) * (1.0 / NFFT)
        down = jnp.where(iota((high, LANES), 0) == j, freq, down)
        along = jnp.where(lane == j, freq, along)
    for q in range(NFFT // LANES):
        turns = down * (iota((high, LANES), 1) + LANES * q).astype(jnp.float32)
        table[0, q] = cos_turns(turns)
        table[1, q] = cos_turns(turns + 0.25)
    turns = (sub & 1).astype(jnp.float32) * 0.25 - along * start.astype(jnp.float32)
    cos_part, sin_part = cos_turns(turns), cos_turns(turns + 0.25)
    for j in range(freqs):
        phase[0, j] = jnp.broadcast_to(cos_part[:, j : j + 1], tile)
        phase[1, j] = jnp.broadcast_to(sin_part[:, j : j + 1], tile)

    weights = []
    for q in range(rows // LANES):
        times = lane + LANES * q - start
        hann = 0.5 - 0.5 * cos_turns(times.astype(jnp.float32) * (1.0 / NFFT))
        scale = scales_ref[pl.ds(LANES * q, LANES)]
        inside = (times >= 0) & (times < NFFT)
        weight = jnp.where(inside, hann * scale[None, :], 0.0)
        weights.append(weight * (1.0 / math.sqrt(NFFT)))

    @pl.loop(0, freqs // 2)
    def _(pair):
        for q in range(rows // LANES):
            turn = q % (NFFT // LANES)
            parts = []
            for j in (2 * pair, 2 * pair + 1):
                cosine = table[0, turn, pl.ds(j, 1), :]
                sine = table[1, turn, pl.ds(j, 1), :]
                value = cosine * phase[0, j] - sine * phase[1, j]
                parts.append(value * weights[q])
            both = jnp.concatenate(parts, 0).astype(jnp.bfloat16)
            coef[pl.ds(pl.multiple_of(pair * 16, 16), 16), pl.ds(LANES * q, LANES)] = both


def gather_kernel(
    sides, zs, total_points,
    snaps_hbm, scales_hbm, offs_hbm, freq_hbm,
    xy, gram_ref,
    snaps, scales_ref, offs_ref, freq_ref, coef, table, phase, send, recv, rows32,
    x_buf, y_buf,
    load_sems, send_sems, recv_sems, gsend_sems, grecv_sems,
):
    ys, xs = sides
    z = lax.axis_index("blk")
    s = lax.axis_index("space")
    core = lax.rem(s, 2)
    x = lax.rem(s // 2, xs)
    y = s // (2 * xs)

    loads = [
        pltpu.make_async_copy(source, target, load_sems.at[i])
        for i, (source, target) in enumerate(
            [
                (scales_hbm, scales_ref),
                (offs_hbm, offs_ref),
                (freq_hbm, freq_ref),
                (snaps_hbm, snaps),
            ]
        )
    ]
    for load in loads:
        load.start()

    def space_of(yy, xx, cc):
        return (yy * xs + xx) * 2 + cc

    z_peers = [lax.rem(z + d, zs) for d in range(1, zs)]
    def far_first(n):
        return sorted(range(1, n), key=lambda d: -min(d, n - d))

    cores = (core, 1 - core)
    x_peers = [space_of(y, lax.rem(x + d, xs), c) for d in far_first(xs) for c in cores]
    x_peers.append(space_of(y, x, 1 - core))
    y_peers = [space_of(lax.rem(y + d, ys), x, core) for d in far_first(ys)]

    barrier = pltpu.get_barrier_semaphore()
    order = far_first(zs)
    for d in order:
        peer = z_peers[d - 1]
        pl.semaphore_signal(barrier, inc=1, device_id={"blk": peer}, device_id_type=MESH)
    for peer in x_peers + y_peers:
        pl.semaphore_signal(barrier, inc=1, device_id={"space": peer}, device_id_type=MESH)

    for load in loads[:3]:
        load.wait()
    write_coeffs(scales_ref, offs_ref, freq_ref, coef, table, phase)
    loads[3].wait()
    width = recv.shape[3]
    copies = []
    for h in range(PARTS):
        spectra = jnp.dot(
            coef[...], snaps[:, width * h : width * (h + 1)], preferred_element_type=jnp.float32
        )
        send[h] = spectra.reshape(send.shape[1:]).astype(jnp.bfloat16)
        recv[h, z] = send[h, z]
        if h == 0:
            pl.semaphore_wait(barrier, len(z_peers) + len(x_peers) + len(y_peers))
        for d in order:
            peer = z_peers[d - 1]
            copy = pltpu.make_async_remote_copy(
                src_ref=send.at[h, peer],
                dst_ref=recv.at[h, z],
                send_sem=send_sems.at[h, d],
                recv_sem=recv_sems.at[h, d],
                device_id={"blk": peer},
                device_id_type=MESH,
            )
            copy.start()
            copies.append(copy)

    half = zs * TILE // 2
    gram = jnp.zeros((half, 2 * half), jnp.float32)
    for h in range(PARTS):
        for copy in copies[(zs - 1) * h : (zs - 1) * (h + 1)]:
            copy.wait_recv()
        chunks = range(width // LANES)
        for q in chunks:
            part = recv[h, :, :, LANES * q : LANES * (q + 1)].astype(jnp.float32)
            rows32[h, q] = part.reshape(2 * half, LANES)

        def every_other(first):
            parts = [rows32[h, q, pl.ds(first, half, stride=2), :] for q in chunks]
            return jnp.concatenate(parts, 1).astype(jnp.bfloat16)

        re, im = every_other(0), every_other(1)
        left = jnp.concatenate([re, im], 1)
        right = jnp.concatenate([left, jnp.concatenate([im, -re], 1)], 0)
        gram += lax.dot_general(
            left, right, (((1,), (1,)), ((), ())), preferred_element_type=jnp.float32
        )
        xy[pl.ds(0, half), pl.ds(width * h, width)] = re
        xy[pl.ds(half, half), pl.ds(width * h, width)] = im

    row, lane = iota(gram.shape, 0), iota(gram.shape, 1)
    packed = jnp.where(lane >= row, gram, pltpu.roll(gram, half, 1))
    upper, lower = packed[: half // 2], pltpu.roll(packed[half // 2 :], half, 1)
    x_buf[x * 2 + core] = jnp.where(iota(upper.shape, 1) < half, upper, lower)

    def exchange(buf, here, peers, base):
        moves = []
        for i, peer in enumerate(peers):
            move = pltpu.make_async_remote_copy(
                src_ref=buf.at[here],
                dst_ref=buf.at[here],
                send_sem=gsend_sems.at[base + i],
                recv_sem=grecv_sems.at[base + i],
                device_id={"space": peer},
                device_id_type=MESH,
            )
            move.start()
            moves.append(move)
        return moves

    def summed(buf, moves):
        for move in moves:
            move.wait_recv()
        total = buf[0]
        for i in range(1, buf.shape[0]):
            total = total + buf[i]
        return total

    moves_x = exchange(x_buf, x * 2 + core, x_peers, 0)
    y_buf[y] = summed(x_buf, moves_x)
    moves_y = exchange(y_buf, y, y_peers, 2 * xs)
    for copy in copies + moves_x:
        copy.wait_send()
    gram_ref[...] = summed(y_buf, moves_y) * (1.0 / total_points)
    for move in moves_y:
        move.wait_send()


def gather_call(snapshots, scales, offsets, freqs, *, space, zs):
    sides = sides_of(space)
    rows, points = snapshots.shape
    cols = zs * TILE
    width = points // PARTS
    kernel = functools.partial(gather_kernel, sides, zs, points * space)
    gram_shape = (cols // 4, cols)
    vmem = pl.BlockSpec(memory_space=pltpu.VMEM)
    anywhere = pl.BlockSpec(memory_space=pl.ANY)
    high = (zs + TILE - 1) // TILE * TILE
    return pl.pallas_call(
        kernel,
        out_shape=(
            pltpu.VMEM((cols, points), jnp.bfloat16),
            pltpu.VMEM(gram_shape, jnp.float32),
        ),
        in_specs=[anywhere] * 4,
        out_specs=(vmem, vmem),
        scratch_shapes=[
            pltpu.VMEM(snapshots.shape, jnp.bfloat16),
            pltpu.VMEM(scales.shape, jnp.float32),
            pltpu.SMEM(offsets.shape, jnp.int32),
            pltpu.SMEM(freqs.shape, jnp.int32),
            pltpu.VMEM((zs * TILE, rows), jnp.bfloat16),
            pltpu.VMEM((2, NFFT // LANES, high, LANES), jnp.float32),
            pltpu.VMEM((2, zs, TILE, LANES), jnp.float32),
            pltpu.VMEM((PARTS, zs, TILE, width), jnp.bfloat16),
            pltpu.VMEM((PARTS, zs, TILE, width), jnp.bfloat16),
            pltpu.VMEM((PARTS, width // LANES, cols, LANES), jnp.float32),
            pltpu.VMEM((2 * sides[1],) + gram_shape, jnp.float32),
            pltpu.VMEM((sides[0],) + gram_shape, jnp.float32),
            pltpu.SemaphoreType.DMA((4,)),
            pltpu.SemaphoreType.DMA((PARTS, zs)),
            pltpu.SemaphoreType.DMA((PARTS, zs)),
            pltpu.SemaphoreType.DMA((2 * sides[1] + sides[0],)),
            pltpu.SemaphoreType.DMA((2 * sides[1] + sides[0],)),
        ],
        compiler_params=pltpu.CompilerParams(collective_id=0, has_side_effects=True),
        name="spectra_and_gram",
    )(snapshots, scales, offsets, freqs)


def unpacked(packed, n):
    both = jnp.concatenate([packed, pltpu.roll(packed, n, 1)], 0)
    flipped = both.T[:n, :]
    row, lane = iota((n, n), 0), iota((n, n), 1)
    both = both[:, :n]
    real = jnp.where(lane >= row, both, flipped)
    imag = jnp.where(lane < row, both, jnp.where(lane > row, -flipped, 0.0))
    return real, imag


def in_three(value):
    high = value.astype(jnp.bfloat16)
    rest = value - high.astype(jnp.float32)
    middle = rest.astype(jnp.bfloat16)
    low = (rest - middle.astype(jnp.float32)).astype(jnp.bfloat16)
    return high, middle, low


def factor_kernel(xy, packed_ref, modes_ref, r_ref, w_ref):
    width = packed_ref.shape[1]
    n = width // 2
    tiles = n // TILE
    real, imag = unpacked(packed_ref[...], n)
    lane, sub = iota((TILE, width), 1), iota((TILE, width), 0)

    def spread(value, row):
        return jnp.take_along_axis(value, jnp.full((TILE, width), row, jnp.int32), 0, mode="promise_in_bounds")

    def across(value, column):
        return jnp.broadcast_to(value[:, column : column + 1], (TILE, width))

    ps, qs = [], []
    for i in range(tiles):
        rows = slice(TILE * i, TILE * (i + 1))
        unit = jnp.where(iota((TILE, n), 1) == iota((TILE, n), 0) + TILE * i, 1.0, 0.0)
        ps.append(jnp.concatenate([real[rows], unit], 1))
        qs.append(jnp.concatenate([imag[rows], jnp.zeros((TILE, n), jnp.float32)], 1))

    for panel in range(tiles):
        group = [panel] + ([panel + 1] if panel + 1 < tiles else [])
        res = {i: [across(ps[i], TILE * panel + j) for j in range(TILE)] for i in group}
        ims = {i: [across(qs[i], TILE * panel + j) for j in range(TILE)] for i in group}
        scale = jnp.zeros((TILE, width), jnp.float32)
        for k in range(TILE):
            pivot = spread(res[panel][k], k)
            inverse = 1.0 / pivot
            scale = jnp.where(sub == k, lax.rsqrt(pivot), scale)
            mults = {i: (res[i][k] * inverse, ims[i][k] * inverse) for i in group}
            for j in range(k + 1, TILE):
                pr, pi = spread(res[panel][j], k), spread(ims[panel][j], k)
                for i in group:
                    mr, mi = mults[i]
                    res[i][j] = res[i][j] - (mr * pr - mi * pi)
                    ims[i][j] = ims[i][j] - (mr * pi + mi * pr)
            p_row, q_row = spread(ps[panel], k), spread(qs[panel], k)
            for i in group:
                mr, mi = mults[i]
                if i == panel:
                    mr, mi = jnp.where(sub > k, mr, 0.0), jnp.where(sub > k, mi, 0.0)
                ps[i] = ps[i] - (mr * p_row - mi * q_row)
                qs[i] = qs[i] - (mr * q_row + mi * p_row)
        p_rows = ps[panel] * scale
        q_rows = qs[panel] * scale
        if panel + 2 < tiles:
            parts_p, parts_q = in_three(p_rows), in_three(q_rows)
            lhs, rhs = [], []
            for i, j in ((0, 0), (0, 1), (1, 0), (0, 2), (2, 0), (1, 1)):
                lhs += [parts_p[i], parts_q[i]]
                rhs.append(jnp.concatenate([parts_p[j], parts_q[j]], 1))
                rhs.append(jnp.concatenate([parts_q[j], -parts_p[j]], 1))
            update = lax.dot_general(
                jnp.concatenate(lhs, 0)[:, :n],
                jnp.concatenate(rhs, 0),
                (((0,), (0,)), ((), ())),
                preferred_element_type=jnp.float32,
            )
            for i in range(panel + 2, tiles):
                part = update[TILE * i : TILE * (i + 1), :]
                ps[i] = ps[i] - part[:, :width]
                qs[i] = qs[i] - part[:, width:]
        row = sub + TILE * panel
        here = pl.ds(TILE * panel, TILE)
        r_ref[0, here, :] = jnp.where(lane >= row, p_rows, 0.0)[:, :n]
        r_ref[1, here, :] = jnp.where(lane > row, q_rows, 0.0)[:, :n]
        even = jnp.where(lane < n, pltpu.roll(p_rows, n, 1), q_rows)
        odd = jnp.where(lane < n, -pltpu.roll(q_rows, n, 1), p_rows)
        w_ref[pl.ds(2 * TILE * panel, TILE, stride=2), :] = even
        w_ref[pl.ds(2 * TILE * panel + 1, TILE, stride=2), :] = odd

    w = w_ref[...]
    high = w.astype(jnp.bfloat16)
    low = (w - high.astype(jnp.float32)).astype(jnp.bfloat16)
    points = xy[...]
    dims = (((0,), (1,)), ((), ()))
    modes = lax.dot_general(points, high, dims, preferred_element_type=jnp.float32)
    modes += lax.dot_general(points, low, dims, preferred_element_type=jnp.float32)
    modes_ref[...] = modes


def factor_call(xy, packed):
    width = packed.shape[1]
    n = width // 2
    vmem = pl.BlockSpec(memory_space=pltpu.VMEM)
    return pl.pallas_call(
        factor_kernel,
        out_shape=(
            jax.ShapeDtypeStruct((xy.shape[1], width), jnp.float32),
            jax.ShapeDtypeStruct((2, n, n), jnp.float32),
        ),
        in_specs=[vmem, vmem],
        out_specs=(vmem, vmem),
        scratch_shapes=[
            pltpu.VMEM((width, width), jnp.float32),
        ],
        name="factor_and_modes",
    )(xy, packed)


def local(space, zs, snapshots, row_scales, block_offsets, freq_index):
    xy, packed = gather_call(
        snapshots, row_scales, block_offsets, freq_index, space=space, zs=zs
    )
    xy = pltpu.with_memory_space_constraint(xy, pltpu.VMEM)
    packed = pltpu.with_memory_space_constraint(packed, pltpu.VMEM)
    modes, r_factor = factor_call(xy, packed)
    return (modes[None], r_factor[None])


def solution(mesh):
    return jax.shard_map(
        functools.partial(local, mesh.shape["space"], mesh.shape["blk"]),
        mesh=mesh,
        in_specs=(P("blk", "space"), P("blk"), P("blk"), P()),
        out_specs=(P("blk", "space", None), P("blk", None, None, None)),
        check_vma=False,
    )
```

```python
import functools
import math

import jax
import jax.numpy as jnp
from jax import lax
from jax.experimental import pallas as pl
from jax.experimental.pallas import tpu as pltpu
from jax.sharding import PartitionSpec as P

NFFT = 512
TILE = 8
LANES = 128
PARTS = 1
MESH = pl.DeviceIdType.MESH


def cos_turns(turns):
    frac = turns - jnp.floor(turns + 0.5)
    half = frac * math.pi
    sq = half * half
    poly = 1.0 + sq * (
        -1.0 / 6
        + sq
        * (
            1.0 / 120
            + sq * (-1.0 / 5040 + sq * (1.0 / 362880 + sq * (-1.0 / 39916800 + sq * (1.0 / 6227020800))))
        )
    )
    sine = half * poly
    return 1.0 - 2.0 * (sine * sine)


def sides_of(space):
    side = {32: 4, 8: 2, 2: 1}[space]
    return side, side


def iota(shape, axis):
    return lax.broadcasted_iota(jnp.int32, shape, axis)


def write_coeffs(scales_ref, offs_ref, freq_ref, coef, table, phase):
    rows = scales_ref.shape[0]
    freqs = freq_ref.shape[0]
    tile = (TILE, LANES)
    sub, lane = iota(tile, 0), iota(tile, 1)
    start = jnp.full(tile, offs_ref[0], jnp.int32)
    for b in range(1, TILE // 2):
        start = jnp.where(sub >= 2 * b, offs_ref[b], start)

    high = (freqs + TILE - 1) // TILE * TILE
    down = jnp.zeros((high, LANES), jnp.float32)
    along = jnp.zeros(tile, jnp.float32)
    for j in range(freqs):
        freq = freq_ref[j].astype(jnp.float32) * (1.0 / NFFT)
        down = jnp.where(iota((high, LANES), 0) == j, freq, down)
        along = jnp.where(lane == j, freq, along)
    for q in range(NFFT // LANES):
        turns = down * (iota((high, LANES), 1) + LANES * q).astype(jnp.float32)
        table[0, q] = cos_turns(turns)
        table[1, q] = cos_turns(turns + 0.25)
    turns = (sub & 1).astype(jnp.float32) * 0.25 - along * start.astype(jnp.float32)
    cos_part, sin_part = cos_turns(turns), cos_turns(turns + 0.25)
    for j in range(freqs):
        phase[0, j] = jnp.broadcast_to(cos_part[:, j : j + 1], tile)
        phase[1, j] = jnp.broadcast_to(sin_part[:, j : j + 1], tile)

    weights = []
    for q in range(rows // LANES):
        times = lane + LANES * q - start
        hann = 0.5 - 0.5 * cos_turns(times.astype(jnp.float32) * (1.0 / NFFT))
        scale = scales_ref[pl.ds(LANES * q, LANES)]
        inside = (times >= 0) & (times < NFFT)
        weight = jnp.where(inside, hann * scale[None, :], 0.0)
        weights.append(weight * (1.0 / math.sqrt(NFFT)))

    @pl.loop(0, freqs // 2)
    def _(pair):
        for q in range(rows // LANES):
            turn = q % (NFFT // LANES)
            parts = []
            for j in (2 * pair, 2 * pair + 1):
                cosine = table[0, turn, pl.ds(j, 1), :]
                sine = table[1, turn, pl.ds(j, 1), :]
                value = cosine * phase[0, j] - sine * phase[1, j]
                parts.append(value * weights[q])
            both = jnp.concatenate(parts, 0).astype(jnp.bfloat16)
            coef[pl.ds(pl.multiple_of(pair * 16, 16), 16), pl.ds(LANES * q, LANES)] = both


def gather_kernel(
    sides, zs, total_points,
    snaps_hbm, scales_hbm, offs_hbm, freq_hbm,
    xy, gram_ref,
    snaps, scales_ref, offs_ref, freq_ref, coef, table, phase, send, recv, rows32,
    x_buf, y_buf,
    load_sems, send_sems, recv_sems, gsend_sems, grecv_sems,
):
    ys, xs = sides
    z = lax.axis_index("blk")
    s = lax.axis_index("space")

    z_peers = [lax.rem(z + d, zs) for d in range(1, zs)]

    def far_first(n):
        return sorted(range(1, n), key=lambda d: -min(d, n - d))

    barrier = pltpu.get_barrier_semaphore()
    order = far_first(zs)
    for d in order:
        peer = z_peers[d - 1]
        pl.semaphore_signal(barrier, inc=1, device_id={"blk": peer}, device_id_type=MESH)

    loads = [
        pltpu.make_async_copy(source, target, load_sems.at[i])
        for i, (source, target) in enumerate(
            [
                (scales_hbm, scales_ref),
                (offs_hbm, offs_ref),
                (freq_hbm, freq_ref),
                (snaps_hbm, snaps),
            ]
        )
    ]
    for load in loads:
        load.start()

    core = lax.rem(s, 2)
    x = lax.rem(s // 2, xs)
    y = s // (2 * xs)

    def space_of(yy, xx, cc):
        return (yy * xs + xx) * 2 + cc

    cores = (core, 1 - core)
    x_peers = [space_of(y, lax.rem(x + d, xs), c) for d in far_first(xs) for c in cores]
    x_peers.append(space_of(y, x, 1 - core))
    y_peers = [space_of(lax.rem(y + d, ys), x, core) for d in far_first(ys)]

    for peer in x_peers + y_peers:
        pl.semaphore_signal(barrier, inc=1, device_id={"space": peer}, device_id_type=MESH)

    for load in loads[:3]:
        load.wait()
    write_coeffs(scales_ref, offs_ref, freq_ref, coef, table, phase)
    loads[3].wait()
    width = recv.shape[3]
    copies = []
    for h in range(PARTS):
        spectra = jnp.dot(
            coef[...], snaps[:, width * h : width * (h + 1)], preferred_element_type=jnp.float32
        )
        send[h] = spectra.reshape(send.shape[1:]).astype(jnp.bfloat16)
        recv[h, z] = send[h, z]
        if h == 0:
            pl.semaphore_wait(barrier, len(z_peers) + len(x_peers) + len(y_peers))
        for d in order:
            peer = z_peers[d - 1]
            copy = pltpu.make_async_remote_copy(
                src_ref=send.at[h, peer],
                dst_ref=recv.at[h, z],
                send_sem=send_sems.at[h, d],
                recv_sem=recv_sems.at[h, d],
                device_id={"blk": peer},
                device_id_type=MESH,
            )
            copy.start()
            copies.append(copy)

    half = zs * TILE // 2
    gram = jnp.zeros((half, 2 * half), jnp.float32)
    for h in range(PARTS):
        for copy in copies[(zs - 1) * h : (zs - 1) * (h + 1)]:
            copy.wait_recv()
        chunks = range(width // LANES)
        for q in chunks:
            part = recv[h, :, :, LANES * q : LANES * (q + 1)].astype(jnp.float32)
            rows32[h, q] = part.reshape(2 * half, LANES)

        def every_other(first):
            parts = [rows32[h, q, pl.ds(first, half, stride=2), :] for q in chunks]
            return jnp.concatenate(parts, 1).astype(jnp.bfloat16)

        re, im = every_other(0), every_other(1)
        left = jnp.concatenate([re, im], 1)
        right = jnp.concatenate([left, jnp.concatenate([im, -re], 1)], 0)
        gram += lax.dot_general(
            left, right, (((1,), (1,)), ((), ())), preferred_element_type=jnp.float32
        )
        xy[pl.ds(0, half), pl.ds(width * h, width)] = re
        xy[pl.ds(half, half), pl.ds(width * h, width)] = im

    row, lane = iota(gram.shape, 0), iota(gram.shape, 1)
    packed = jnp.where(lane >= row, gram, pltpu.roll(gram, half, 1))
    upper, lower = packed[: half // 2], pltpu.roll(packed[half // 2 :], half, 1)
    x_buf[x * 2 + core] = jnp.where(iota(upper.shape, 1) < half, upper, lower)

    def exchange(buf, here, peers, base):
        moves = []
        for i, peer in enumerate(peers):
            move = pltpu.make_async_remote_copy(
                src_ref=buf.at[here],
                dst_ref=buf.at[here],
                send_sem=gsend_sems.at[base + i],
                recv_sem=grecv_sems.at[base + i],
                device_id={"space": peer},
                device_id_type=MESH,
            )
            move.start()
            moves.append(move)
        return moves

    def summed(buf, moves):
        for move in moves:
            move.wait_recv()
        total = buf[0]
        for i in range(1, buf.shape[0]):
            total = total + buf[i]
        return total

    moves_x = exchange(x_buf, x * 2 + core, x_peers, 0)
    y_buf[y] = summed(x_buf, moves_x)
    moves_y = exchange(y_buf, y, y_peers, 2 * xs)
    for copy in copies + moves_x:
        copy.wait_send()
    gram_ref[...] = summed(y_buf, moves_y) * (1.0 / total_points)
    for move in moves_y:
        move.wait_send()


def gather_call(snapshots, scales, offsets, freqs, *, space, zs):
    sides = sides_of(space)
    rows, points = snapshots.shape
    cols = zs * TILE
    width = points // PARTS
    kernel = functools.partial(gather_kernel, sides, zs, points * space)
    gram_shape = (cols // 4, cols)
    vmem = pl.BlockSpec(memory_space=pltpu.VMEM)
    anywhere = pl.BlockSpec(memory_space=pl.ANY)
    high = (zs + TILE - 1) // TILE * TILE
    return pl.pallas_call(
        kernel,
        out_shape=(
            pltpu.VMEM((cols, points), jnp.bfloat16),
            pltpu.VMEM(gram_shape, jnp.float32),
        ),
        in_specs=[anywhere] * 4,
        out_specs=(vmem, vmem),
        scratch_shapes=[
            pltpu.VMEM(snapshots.shape, jnp.bfloat16),
            pltpu.VMEM(scales.shape, jnp.float32),
            pltpu.SMEM(offsets.shape, jnp.int32),
            pltpu.SMEM(freqs.shape, jnp.int32),
            pltpu.VMEM((zs * TILE, rows), jnp.bfloat16),
            pltpu.VMEM((2, NFFT // LANES, high, LANES), jnp.float32),
            pltpu.VMEM((2, zs, TILE, LANES), jnp.float32),
            pltpu.VMEM((PARTS, zs, TILE, width), jnp.bfloat16),
            pltpu.VMEM((PARTS, zs, TILE, width), jnp.bfloat16),
            pltpu.VMEM((PARTS, width // LANES, cols, LANES), jnp.float32),
            pltpu.VMEM((2 * sides[1],) + gram_shape, jnp.float32),
            pltpu.VMEM((sides[0],) + gram_shape, jnp.float32),
            pltpu.SemaphoreType.DMA((4,)),
            pltpu.SemaphoreType.DMA((PARTS, zs)),
            pltpu.SemaphoreType.DMA((PARTS, zs)),
            pltpu.SemaphoreType.DMA((2 * sides[1] + sides[0],)),
            pltpu.SemaphoreType.DMA((2 * sides[1] + sides[0],)),
        ],
        compiler_params=pltpu.CompilerParams(collective_id=0, has_side_effects=True),
        name="spectra_and_gram",
    )(snapshots, scales, offsets, freqs)


def unpacked(packed, n):
    both = jnp.concatenate([packed, pltpu.roll(packed, n, 1)], 0)
    flipped = both.T[:n, :]
    row, lane = iota((n, n), 0), iota((n, n), 1)
    both = both[:, :n]
    real = jnp.where(lane >= row, both, flipped)
    imag = jnp.where(lane < row, both, jnp.where(lane > row, -flipped, 0.0))
    return real, imag


def in_three(value):
    high = value.astype(jnp.bfloat16)
    rest = value - high.astype(jnp.float32)
    middle = rest.astype(jnp.bfloat16)
    low = (rest - middle.astype(jnp.float32)).astype(jnp.bfloat16)
    return high, middle, low


def factor_kernel(xy, packed_ref, modes_ref, r_ref, w_ref):
    width = packed_ref.shape[1]
    n = width // 2
    tiles = n // TILE
    real, imag = unpacked(packed_ref[...], n)
    lane, sub = iota((TILE, width), 1), iota((TILE, width), 0)

    def spread(value, row):
        return jnp.take_along_axis(value, jnp.full((TILE, width), row, jnp.int32), 0, mode="promise_in_bounds")

    def across(value, column):
        return jnp.broadcast_to(value[:, column : column + 1], (TILE, width))

    ps, qs = [], []
    for i in range(tiles):
        rows = slice(TILE * i, TILE * (i + 1))
        unit = jnp.where(iota((TILE, n), 1) == iota((TILE, n), 0) + TILE * i, 1.0, 0.0)
        ps.append(jnp.concatenate([real[rows], unit], 1))
        qs.append(jnp.concatenate([imag[rows], jnp.zeros((TILE, n), jnp.float32)], 1))

    for panel in range(tiles):
        group = [panel] + ([panel + 1] if panel + 1 < tiles else [])
        res = {i: [across(ps[i], TILE * panel + j) for j in range(TILE)] for i in group}
        ims = {i: [across(qs[i], TILE * panel + j) for j in range(TILE)] for i in group}
        scale = jnp.zeros((TILE, width), jnp.float32)
        for k in range(TILE):
            pivot = spread(res[panel][k], k)
            inverse = 1.0 / pivot
            scale = jnp.where(sub == k, lax.rsqrt(pivot), scale)
            mults = {i: (res[i][k] * inverse, ims[i][k] * inverse) for i in group}
            for j in range(k + 1, TILE):
                pr, pi = spread(res[panel][j], k), spread(ims[panel][j], k)
                for i in group:
                    mr, mi = mults[i]
                    res[i][j] = res[i][j] - (mr * pr - mi * pi)
                    ims[i][j] = ims[i][j] - (mr * pi + mi * pr)
            p_row, q_row = spread(ps[panel], k), spread(qs[panel], k)
            for i in group:
                mr, mi = mults[i]
                if i == panel:
                    mr, mi = jnp.where(sub > k, mr, 0.0), jnp.where(sub > k, mi, 0.0)
                ps[i] = ps[i] - (mr * p_row - mi * q_row)
                qs[i] = qs[i] - (mr * q_row + mi * p_row)
        p_rows = ps[panel] * scale
        q_rows = qs[panel] * scale
        if panel + 2 < tiles:
            parts_p, parts_q = in_three(p_rows), in_three(q_rows)
            lhs, rhs = [], []
            for i, j in ((0, 0), (0, 1), (1, 0), (0, 2), (2, 0), (1, 1)):
                lhs += [parts_p[i], parts_q[i]]
                rhs.append(jnp.concatenate([parts_p[j], parts_q[j]], 1))
                rhs.append(jnp.concatenate([parts_q[j], -parts_p[j]], 1))
            update = lax.dot_general(
                jnp.concatenate(lhs, 0)[:, :n],
                jnp.concatenate(rhs, 0),
                (((0,), (0,)), ((), ())),
                preferred_element_type=jnp.float32,
            )
            for i in range(panel + 2, tiles):
                part = update[TILE * i : TILE * (i + 1), :]
                ps[i] = ps[i] - part[:, :width]
                qs[i] = qs[i] - part[:, width:]
        row = sub + TILE * panel
        here = pl.ds(TILE * panel, TILE)
        r_ref[0, here, :] = jnp.where(lane >= row, p_rows, 0.0)[:, :n]
        r_ref[1, here, :] = jnp.where(lane > row, q_rows, 0.0)[:, :n]
        even = jnp.where(lane < n, pltpu.roll(p_rows, n, 1), q_rows)
        odd = jnp.where(lane < n, -pltpu.roll(q_rows, n, 1), p_rows)
        w_ref[pl.ds(2 * TILE * panel, TILE, stride=2), :] = even
        w_ref[pl.ds(2 * TILE * panel + 1, TILE, stride=2), :] = odd

    w = w_ref[...]
    high = w.astype(jnp.bfloat16)
    low = (w - high.astype(jnp.float32)).astype(jnp.bfloat16)
    points = xy[...]
    dims = (((0,), (1,)), ((), ()))
    modes = lax.dot_general(points, high, dims, preferred_element_type=jnp.float32)
    modes += lax.dot_general(points, low, dims, preferred_element_type=jnp.float32)
    modes_ref[...] = modes


def factor_call(xy, packed):
    width = packed.shape[1]
    n = width // 2
    vmem = pl.BlockSpec(memory_space=pltpu.VMEM)
    return pl.pallas_call(
        factor_kernel,
        out_shape=(
            jax.ShapeDtypeStruct((xy.shape[1], width), jnp.float32),
            jax.ShapeDtypeStruct((2, n, n), jnp.float32),
        ),
        in_specs=[vmem, vmem],
        out_specs=(vmem, vmem),
        scratch_shapes=[
            pltpu.VMEM((width, width), jnp.float32),
        ],
        name="factor_and_modes",
    )(xy, packed)


def local(space, zs, snapshots, row_scales, block_offsets, freq_index):
    xy, packed = gather_call(
        snapshots, row_scales, block_offsets, freq_index, space=space, zs=zs
    )
    xy = pltpu.with_memory_space_constraint(xy, pltpu.VMEM)
    packed = pltpu.with_memory_space_constraint(packed, pltpu.VMEM)
    modes, r_factor = factor_call(xy, packed)
    return (modes[None], r_factor[None])


def solution(mesh):
    return jax.shard_map(
        functools.partial(local, mesh.shape["space"], mesh.shape["blk"]),
        mesh=mesh,
        in_specs=(P("blk", "space"), P("blk"), P("blk"), P()),
        out_specs=(P("blk", "space", None), P("blk", None, None, None)),
        check_vma=False,
    )
```
